32 devices in a mesh: pipe: 2 (over core), seq: 8 (over z, x), tp: 2 (over y).
Axes of the slice: x: 2, y: 2, z: 4, core: 2. Of those that a mesh axis runs over, the one named last changes fastest.
Arguments:
- hidden_in: bfloat16 [1, 4096, 2560], P(None, ('seq', 'tp')), may hold values from -6 to 6
- doc_ids: int32 [1, 4096], P(None, 'seq'), may hold values from 0 to 1, never falling along the last dimension, each value on 1 to 3072 neighbouring positions
- norm_gain: float32 [2, 2560], P('pipe'), may hold values from 0.1 to 1.9
- in_zx: bfloat16 [2, 2560, 2, 5120], P('pipe', None, None, 'tp'), may hold values from -0.125 to 0.125
- in_bc: bfloat16 [2, 2560, 256], P('pipe'), may hold values from -0.125 to 0.125
- in_dt: bfloat16 [2, 2560, 80], P('pipe', None, 'tp'), may hold values from -0.125 to 0.125
- conv_x: float32 [2, 4, 5120], P('pipe', None, 'tp'), may hold values from -3 to 3
- conv_bc: float32 [2, 4, 256], P('pipe'), may hold values from -3 to 3
- bias_x: float32 [2, 5120], P('pipe', 'tp'), may hold values from -3 to 3
- bias_bc: float32 [2, 256], P('pipe'), may hold values from -3 to 3
- dt_bias: float32 [2, 80], P('pipe', 'tp'), may hold values from -2 to 1
- a_log: float32 [2, 80], P('pipe', 'tp'), may hold values from -12 to 0, as said below
- d_skip: float32 [2, 80], P('pipe', 'tp'), may hold values from 0.5 to 1.5
- gated_gain: float32 [2, 5120], P('pipe', 'tp'), may hold values from 0.1 to 1.9
- out_w: bfloat16 [2, 5120, 2560], P('pipe', 'tp'), may hold values from -0.078125 to 0.078125
Outputs:
- section_out: bfloat16 [2, 1, 4096, 2560], P('pipe', None, ('seq', 'tp'))
The draws below stay inside these ranges and needn't reach their ends.
Inputs may be any that keep to these rules, and one draw needn't show every extreme that they name: `doc_ids`: in each row the document numbers start at 0, never fall, and rise by one where a new document begins; every document spans 1 to 3072 positions. `a_log`: logarithms of rates between 0.5 / 4096 and 1.
All inputs are finite; a program needn't handle non-finite values.
Results may differ from the reference program's by a relative error of at most 0.02.
Values may be sent and summed in bfloat16 or wider, within the bound.
A program may use at most 192 MiB of HBM per device.

```python
import math
import jax
import jax.numpy as jnp
import numpy as np
from jax import lax

D = 2560
E = 5120
H = 80
HEADDIM = 64
NS = 128
KW = 4
BLOCK = 256
MB = 1
SEQLEN = 4096
LAYERS = 2


def draw_a_log(key, part):
    uniform_draw = jax.random.uniform(key, (LAYERS, H), jnp.float32)
    lowest = math.log(0.5 / SEQLEN)
    return (lowest * (1.0 - uniform_draw)).astype(jnp.float32)


def block_scale(stream_key, extent, pieces, least, high):
    def one(axis_at, blocks):
        steps = jax.random.uniform(jax.random.fold_in(jax.random.fold_in(stream_key, 6), axis_at), (blocks,), jnp.float32, least / len(pieces), high / len(pieces))
        return jnp.repeat(jnp.exp(steps), extent[axis_at] // blocks).reshape((-1,) + (1,) * (len(extent) - axis_at - 1))

    loudness = one(*pieces[0])
    for cut in pieces[1:]:
        loudness = loudness * one(*cut)
    return loudness


def profile(count, total, bound, slope):
    portions = [(1 << 20) // math.isqrt(standing ** slope) + 1 for standing in range(2, count + 1)]
    spare, given = total - bound - (count - 1), [1] * (count - 1)
    while spare > 0:
        movable = [i for i in range(count - 1) if given[i] < bound]
        whole, remaining = sum([portions[i] for i in movable]), spare
        for i in movable:
            addition = min(bound - given[i], max(1, remaining * portions[i] // whole), spare)
            given[i] = given[i] + addition
            spare = spare - addition
    return np.array([bound] + given)


def uneven(own_key, number_of, total, limit, lean):
    if number_of == 2:
        one = jax.random.randint(own_key, (), max(1, total - limit), min(limit, total - 1) + 1)
        return jnp.stack([one, total - one])
    tallies = jnp.asarray(profile(number_of, total, limit, lean), jnp.int32)
    couples = (number_of - 1) // 2
    source_of, taker = tallies[1:1 + 2 * couples:2], tallies[2:2 + 2 * couples:2]
    slack = jnp.minimum(source_of - 1, limit - taker)
    passed = jax.random.randint(jax.random.fold_in(own_key, 1), (couples,), 0, 1 << 20) % (slack + 1)
    tallies = tallies.at[1:1 + 2 * couples:2].set(source_of - passed).at[2:2 + 2 * couples:2].set(taker + passed)
    return tallies[jax.random.permutation(jax.random.fold_in(own_key, 2), number_of)]


def gaussian(key, extent, scale, bound, shards=(), dtype=jnp.bfloat16):
    entries = scale * jax.random.normal(key, extent, jnp.float32)
    if shards:
        entries = entries * block_scale(key, extent, shards, -0.22, 0.18)
    return jnp.clip(entries, -bound, bound).astype(dtype)


def setup_inputs(seed: int = 0) -> dict:
    arg_keys = jax.random.split(jax.random.key(seed), 16)
    hidden_in = gaussian(arg_keys[0], (MB, SEQLEN, D), 1.0, 6.0, ((1, 16),))
    doc_ids = jax.vmap(lambda own: jnp.searchsorted(jnp.cumsum(uneven(own, 2, SEQLEN, 3 * SEQLEN // 4, 0)), jnp.arange(SEQLEN), side="right"))(jax.random.split(arg_keys[1], MB)).reshape((MB, SEQLEN)).astype(jnp.int32)
    norm_gain = jnp.clip(1.0 + 0.18 * jax.random.normal(arg_keys[2], (LAYERS, D), jnp.float32), 0.1, 1.9)
    in_zx = gaussian(arg_keys[3], (LAYERS, D, 2, E), D ** -0.5, 0.125, ((0, 2), (3, 2)))
    in_bc = gaussian(arg_keys[4], (LAYERS, D, 2 * NS), D ** -0.5, 0.125, ((0, 2),))
    in_dt = gaussian(arg_keys[5], (LAYERS, D, H), D ** -0.5, 0.125, ((0, 2), (2, 2)))
    conv_x = gaussian(arg_keys[6], (LAYERS, KW, E), KW ** -0.5, 3.0, ((0, 2), (2, 2)), jnp.float32)
    conv_bc = gaussian(arg_keys[7], (LAYERS, KW, 2 * NS), KW ** -0.5, 3.0, ((0, 2),), jnp.float32)
    bias_x = gaussian(arg_keys[8], (LAYERS, E), 0.5, 3.0, ((0, 2), (1, 2)), jnp.float32)
    bias_bc = gaussian(arg_keys[9], (LAYERS, 2 * NS), 0.5, 3.0, ((0, 2),), jnp.float32)
    dt_bias = jnp.clip(-2.0 + 3.0 * jax.random.uniform(arg_keys[10], (LAYERS, H), jnp.float32) ** block_scale(arg_keys[10], (LAYERS, H), ((0, 2), (1, 2)), -0.2, 0.2), -2.0, 1.0)
    a_log = draw_a_log(jax.random.fold_in(arg_keys[15], 71), 0)
    d_skip = jnp.clip(0.5 + 1.0 * jax.random.uniform(arg_keys[12], (LAYERS, H), jnp.float32) ** block_scale(arg_keys[12], (LAYERS, H), ((0, 2), (1, 2)), -0.2, 0.2), 0.5, 1.5)
    gated_gain = jnp.clip(1.0 + 0.18 * jax.random.normal(arg_keys[13], (LAYERS, E), jnp.float32), 0.1, 1.9)
    out_w = gaussian(arg_keys[14], (LAYERS, E, D), E ** -0.5, 0.078125, ((0, 2), (1, 2)))
    return dict(hidden_in=hidden_in, doc_ids=doc_ids, norm_gain=norm_gain, in_zx=in_zx, in_bc=in_bc, in_dt=in_dt, conv_x=conv_x, conv_bc=conv_bc, bias_x=bias_x, bias_bc=bias_bc, dt_bias=dt_bias, a_log=a_log, d_skip=d_skip, gated_gain=gated_gain, out_w=out_w)


epsilon = 1e-05
highest = lax.Precision.HIGHEST

def conv_mix(row_block, edge_rows, row_ids, edge_ids, weight, shift_bias):
    padded = jnp.concatenate([edge_rows, row_block], 0)
    padded_ids = jnp.concatenate([edge_ids, row_ids], 0)
    row_count = row_block.shape[0]
    running = jnp.zeros_like(row_block) + shift_bias[None, :]
    for offset in range(weight.shape[0]):
        keep_mask = (padded_ids[offset:offset + row_count] == row_ids).astype(jnp.float32)
        running = running + keep_mask[:, None] * weight[offset][None, :] * padded[offset:offset + row_count]
    return jax.nn.silu(running)

def block_step(state_in, inputs, decay_rates):
    x_block, step_sizes, b_block, c_block, seg_block, prev_id = inputs
    log_decay = jnp.cumsum(step_sizes * decay_rates[:, None], axis=1)
    block_length = seg_block.shape[0]
    causal_mask = jnp.arange(block_length)[:, None] >= jnp.arange(block_length)[None, :]
    same_doc = causal_mask & (seg_block[:, None] == seg_block[None, :])
    spread = log_decay[:, :, None] - log_decay[:, None, :]
    mixing = jnp.where(same_doc[None], jnp.exp(jnp.where(same_doc[None], spread, 0.0)), 0.0)
    gram_matrix = jnp.dot(c_block, b_block.T, precision=highest)
    weights = mixing * gram_matrix[None] * step_sizes[:, None, :]
    outputs = jnp.einsum('hps,hts->hpt', x_block, weights, precision=highest)
    carried = (seg_block == prev_id).astype(jnp.float32)
    outputs = outputs + jnp.exp(log_decay)[:, None, :] * carried[None, None, :] * jnp.einsum('hpn,tn->hpt', state_in, c_block, precision=highest)
    end_weight = jnp.exp(log_decay[:, -1:] - log_decay) * (seg_block == seg_block[-1]).astype(jnp.float32)[None, :] * step_sizes
    fresh_state = jnp.einsum('hps,sn->hpn', x_block * end_weight[:, None, :], b_block, precision=highest)
    keep_all = jnp.exp(log_decay[:, -1]) * (seg_block[-1] == prev_id).astype(jnp.float32)
    return (keep_all[:, None, None] * state_in + fresh_state, outputs)

def mamba_layer(hidden, row_ids, norm_scale, weight_zx, weight_bc, weight_dt, kernel_x, kernel_bc, offset_x, offset_bc, dt_shift, log_rate, skip_scale, gate_scale, weight_out):
    hidden_f = hidden.astype(jnp.float32)
    normed = (hidden_f * lax.rsqrt(lax.optimization_barrier(jnp.mean(hidden_f * hidden_f, axis=1, keepdims=True)) + epsilon) * norm_scale[None, :]).astype(jnp.bfloat16)
    gate_in = jnp.dot(normed, weight_zx[:, 0, :], preferred_element_type=jnp.float32)
    x_raw = jnp.dot(normed, weight_zx[:, 1, :], preferred_element_type=jnp.float32)
    bc_raw = jnp.dot(normed, weight_bc, preferred_element_type=jnp.float32)
    dt_raw = jnp.dot(normed, weight_dt, preferred_element_type=jnp.float32)
    pre_conv = jnp.concatenate([x_raw, bc_raw], 1)
    kernel = jnp.concatenate([kernel_x, kernel_bc], 1)
    kernel_bias = jnp.concatenate([offset_x, offset_bc], 0)
    edge_rows = jnp.zeros((KW - 1, E + 2 * NS), jnp.float32)
    edge_ids = jnp.full((KW - 1,), -1, jnp.int32)
    conv_out = conv_mix(pre_conv, edge_rows, row_ids, edge_ids, kernel, kernel_bias)
    x_heads = conv_out[:, :E].T.reshape(H, HEADDIM, SEQLEN)
    b_conv = conv_out[:, E:E + NS]
    c_conv = conv_out[:, E + NS:]
    step_sizes = jax.nn.softplus(dt_raw + dt_shift[None, :]).T
    decay_rates = -jnp.exp(log_rate)
    blocks = SEQLEN // BLOCK
    prev_ids = jnp.concatenate([row_ids[:1], row_ids[BLOCK - 1:SEQLEN - 1:BLOCK]], 0)
    stacked = (x_heads.reshape(H, HEADDIM, blocks, BLOCK).transpose(2, 0, 1, 3), step_sizes.reshape(H, blocks, BLOCK).transpose(1, 0, 2), b_conv.reshape(blocks, BLOCK, NS), c_conv.reshape(blocks, BLOCK, NS), row_ids.reshape(blocks, BLOCK), prev_ids)

    def scan_body(state_in, inputs):
        return block_step(state_in, inputs, decay_rates)
    final_state, outputs = lax.scan(scan_body, jnp.zeros((H, HEADDIM, NS), jnp.float32), stacked)
    outputs = outputs.transpose(1, 2, 0, 3).reshape(H, HEADDIM, SEQLEN)
    outputs = outputs + skip_scale[:, None, None] * x_heads
    gated_rows = outputs.reshape(E, SEQLEN).T * jax.nn.silu(gate_in)
    branch_in = (gated_rows * lax.rsqrt(lax.optimization_barrier(jnp.mean(gated_rows * gated_rows, axis=1, keepdims=True)) + epsilon) * gate_scale[None, :]).astype(jnp.bfloat16)
    return (hidden_f + jnp.dot(branch_in, weight_out, preferred_element_type=jnp.float32)).astype(jnp.bfloat16)

def reference(hidden_in, doc_ids, norm_gain, in_zx, in_bc, in_dt, conv_x, conv_bc, bias_x, bias_bc, dt_bias, a_log, d_skip, gated_gain, out_w):
    per_layer = [[None] * MB for layer_index in range(LAYERS)]
    for micro_index in range(MB):
        hidden = hidden_in[micro_index]
        row_ids = doc_ids[micro_index]
        for layer_index in range(LAYERS):
            hidden = mamba_layer(hidden, row_ids, norm_gain[layer_index], in_zx[layer_index], in_bc[layer_index], in_dt[layer_index], conv_x[layer_index], conv_bc[layer_index], bias_x[layer_index], bias_bc[layer_index], dt_bias[layer_index], a_log[layer_index], d_skip[layer_index], gated_gain[layer_index], out_w[layer_index])
            per_layer[layer_index][micro_index] = hidden
    return jnp.stack([jnp.stack(micro_list) for micro_list in per_layer])
```

```python
import jax
import jax.numpy as jnp
from jax import lax
from jax.sharding import PartitionSpec as P

BLOCK = 256


epsilon = 1e-05


def narrow_einsum(form, left, right):
    return jnp.einsum(
        form,
        left.astype(jnp.bfloat16),
        right.astype(jnp.bfloat16),
        preferred_element_type=jnp.float32,
    )


def shifted(block, axis, distance):
    devices = range(lax.axis_size(axis))
    route = [(i - distance, i) for i in devices if i - distance in devices]
    return lax.ppermute(block, axis, route)


def live_sections(tick_index, micro_count):
    sections = range(lax.axis_size("pipe"))
    return [p for p in sections if 0 <= tick_index - p < micro_count]


def live_shift(block, axis, distance, live, wrap=False):
    size = lax.axis_size(axis)
    route = []
    for p in live:
        for i in range(size):
            j = i + distance
            if wrap or j < size:
                route.append((p * size + i, p * size + j % size))
    return lax.ppermute(block, ("pipe", axis), route)


def gathered_rows(rows, axis, live):
    size = lax.axis_size(axis)
    place = lax.axis_index(axis)
    count = rows.shape[0]
    whole = jnp.zeros((size * count,) + rows.shape[1:], rows.dtype)
    whole = lax.dynamic_update_slice_in_dim(whole, rows, place * count, 0)
    for step in range(1, size):
        other = live_shift(rows, axis, step, live, True)
        source = lax.rem(place - step + size, size)
        whole = lax.dynamic_update_slice_in_dim(whole, other, source * count, 0)
    return whole


def scattered_sum(rows, axis, live):
    size = lax.axis_size(axis)
    place = lax.axis_index(axis)
    count = rows.shape[0] // size
    total = lax.dynamic_slice_in_dim(rows, place * count, count, 0).astype(jnp.float32)
    for step in range(1, size):
        target = lax.rem(place + step, size)
        piece = lax.dynamic_slice_in_dim(rows, target * count, count, 0).astype(jnp.bfloat16)
        total = total + live_shift(piece, axis, step, live, True).astype(jnp.float32)
    return total


def summed(part, axis, live):
    total = part
    for step in range(1, lax.axis_size(axis)):
        total = total + live_shift(part, axis, step, live, True)
    return total


def pack_carry(keep, state):
    high = keep.astype(jnp.bfloat16)
    low = (keep - high.astype(jnp.float32)).astype(jnp.bfloat16)
    heads, width, states = state.shape
    slab = jnp.pad(jnp.stack([high, low]), ((0, width - 2), (0, states - heads)))
    return jnp.concatenate([state.astype(jnp.bfloat16), slab[None]], 0)


def unpack_carry(packed, heads):
    pair = packed[heads, :2, :heads].astype(jnp.float32)
    return pair[0] + pair[1], packed[:heads].astype(jnp.float32)


def carried_in(keep, state, axis, live):
    heads = keep.shape[0]
    size = lax.axis_size(axis)
    keep, state = unpack_carry(live_shift(pack_carry(keep, state), axis, 1, live), heads)
    distance = 1
    while distance < size - 1:
        earlier = live_shift(pack_carry(keep, state), axis, distance, live)
        before = unpack_carry(earlier, heads)
        keep, state = combine_carry(before, (keep, state))
        distance *= 2
    return state


def conv_mix(row_block, edge_rows, row_ids, edge_ids, weight, shift_bias):
    padded = jnp.concatenate([edge_rows, row_block], 0)
    padded_ids = jnp.concatenate([edge_ids, row_ids], 0)
    row_count = row_block.shape[0]
    running = jnp.zeros_like(row_block) + shift_bias[None, :]
    for offset in range(weight.shape[0]):
        keep_mask = (padded_ids[offset : offset + row_count] == row_ids).astype(jnp.float32)
        running = (
            running
            + keep_mask[:, None] * weight[offset][None, :] * padded[offset : offset + row_count]
        )
    return jax.nn.silu(running)


def block_step(state_in, inputs, decay_rates):
    x_block, step_sizes, b_block, c_block, seg_block, prev_id = inputs
    log_decay = jnp.cumsum(step_sizes * decay_rates[:, None], axis=1)
    block_length = seg_block.shape[0]
    causal_mask = jnp.arange(block_length)[:, None] >= jnp.arange(block_length)[None, :]
    same_doc = causal_mask & (seg_block[:, None] == seg_block[None, :])
    spread = log_decay[:, :, None] - log_decay[:, None, :]
    mixing = jnp.where(same_doc[None], jnp.exp(jnp.where(same_doc[None], spread, 0.0)), 0.0)
    gram_matrix = narrow_einsum("tn,sn->ts", c_block, b_block)
    weights = mixing * gram_matrix[None] * step_sizes[:, None, :]
    outputs = narrow_einsum("hps,hts->hpt", x_block, weights)
    carried = (seg_block == prev_id).astype(jnp.float32)
    if state_in is not None:
        outputs = outputs + jnp.exp(log_decay)[:, None, :] * carried[
            None, None, :
        ] * narrow_einsum("hpn,tn->hpt", state_in, c_block)
    end_weight = (
        jnp.exp(log_decay[:, -1:] - log_decay)
        * (seg_block == seg_block[-1]).astype(jnp.float32)[None, :]
        * step_sizes
    )
    fresh_state = narrow_einsum("hps,sn->hpn", x_block * end_weight[:, None, :], b_block)
    if state_in is None:
        return (fresh_state, outputs)
    keep_all = jnp.exp(log_decay[:, -1]) * (seg_block[-1] == prev_id).astype(jnp.float32)
    return (keep_all[:, None, None] * state_in + fresh_state, outputs)


def combine_carry(earlier, latter):
    return (earlier[0] * latter[0], latter[0][:, None, None] * earlier[1] + latter[1])


def rms_rows(hidden_f, norm_scale):
    return (
        hidden_f
        * lax.rsqrt(jnp.mean(hidden_f * hidden_f, axis=1, keepdims=True) + epsilon)
        * norm_scale[None, :]
    ).astype(jnp.bfloat16)


def project_rows(normed, weight_zx, weight_bc, weight_dt):
    return (
        jnp.dot(normed, weight_zx, preferred_element_type=jnp.float32),
        jnp.dot(normed, weight_bc, preferred_element_type=jnp.float32),
        jnp.dot(normed, weight_dt, preferred_element_type=jnp.float32),
    )


def mixer_block(
    projected, row_ids, kernel, kernel_bias, dt_shift, log_rate, skip_scale, gate_scale, live
):
    local_width = gate_scale.shape[0]
    heads_local = dt_shift.shape[0]
    head_width = local_width // heads_local
    projected_zx, projected_bc, dt_raw = projected
    token_count = projected_zx.shape[0]
    state_width = (kernel.shape[1] - local_width) // 2
    edge_count = kernel.shape[0] - 1
    gate_in = projected_zx[:, :local_width]
    x_raw = projected_zx[:, local_width:]
    edge_begin = token_count - edge_count
    edge_x, edge_bc, edge_ids = live_shift(
        (x_raw[edge_begin:], projected_bc[edge_begin:], row_ids[edge_begin:]), "seq", 1, live
    )
    bc_conv = conv_mix(
        projected_bc, edge_bc, row_ids, edge_ids, kernel[:, local_width:], kernel_bias[local_width:]
    )
    x_conv = conv_mix(
        x_raw, edge_x, row_ids, edge_ids, kernel[:, :local_width], kernel_bias[:local_width]
    )
    x_heads = x_conv.T.reshape(heads_local, head_width, token_count)
    b_conv = bc_conv[:, :state_width]
    c_conv = bc_conv[:, state_width:]
    step_sizes = jax.nn.softplus(dt_raw + dt_shift[None, :]).T
    decay_rates = -jnp.exp(log_rate)
    first_prev = edge_ids[edge_count - 1]
    state_run = None
    pieces = []
    for block_index in range(token_count // BLOCK):
        block_begin = block_index * BLOCK
        block_end = block_begin + BLOCK
        prev_id = first_prev if block_index == 0 else row_ids[block_begin - 1]
        state_run, block_out = block_step(
            state_run,
            (
                x_heads[:, :, block_begin:block_end],
                step_sizes[:, block_begin:block_end],
                b_conv[block_begin:block_end],
                c_conv[block_begin:block_end],
                row_ids[block_begin:block_end],
                prev_id,
            ),
            decay_rates,
        )
        pieces.append(block_out)
    outputs = jnp.concatenate(pieces, 2)
    log_total = jnp.cumsum(step_sizes * decay_rates[:, None], axis=1)
    carried = (row_ids == first_prev).astype(jnp.float32)
    shard_keep = jnp.exp(log_total[:, -1]) * carried[token_count - 1]
    incoming = carried_in(shard_keep, state_run, "seq", live)
    outputs = outputs + jnp.exp(log_total)[:, None, :] * carried[None, None, :] * narrow_einsum(
        "hpn,tn->hpt", incoming, c_conv
    )
    outputs = outputs + skip_scale[:, None, None] * x_heads
    gated_rows = outputs.reshape(local_width, token_count).T * jax.nn.silu(gate_in)
    total_sq = summed(jnp.sum(gated_rows * gated_rows, axis=1), "tp", live)
    full_width = local_width * lax.axis_size("tp")
    return (
        gated_rows * lax.rsqrt(total_sq / full_width + epsilon)[:, None] * gate_scale[None, :]
    ).astype(jnp.bfloat16)


def local(
    hidden_in,
    doc_ids,
    norm_gain,
    in_zx,
    in_bc,
    in_dt,
    conv_x,
    conv_bc,
    bias_x,
    bias_bc,
    dt_bias,
    a_log,
    d_skip,
    gated_gain,
    out_w,
):
    sections = lax.axis_size("pipe")
    section_index = lax.axis_index("pipe")
    micro_count = hidden_in.shape[0]
    local_width = gated_gain.shape[1]
    weight_zx = in_zx[0].reshape(in_zx.shape[1], 2 * local_width)
    weight_bc = in_bc[0]
    weight_dt = in_dt[0]
    kernel = jnp.concatenate([conv_x[0], conv_bc[0]], 1)
    kernel_bias = jnp.concatenate([bias_x[0], bias_bc[0]], 0)
    weight_out = out_w[0]
    saved_slots = [jnp.zeros_like(hidden_in[0])]
    received = jnp.zeros_like(hidden_in[0])
    finished = received
    for tick_index in range(micro_count + sections - 1):
        live = live_sections(tick_index, micro_count)
        if tick_index > 0:
            received = shifted(finished, "pipe", 1)
        fresh_rows = hidden_in[tick_index] if tick_index < micro_count else jnp.zeros_like(received)
        current = jnp.where(section_index == 0, fresh_rows, received)
        micro_index = tick_index - section_index
        row_ids = lax.dynamic_index_in_dim(
            doc_ids, jnp.clip(micro_index, 0, micro_count - 1), 0, keepdims=False
        ).astype(jnp.float32)
        current_f = current.astype(jnp.float32)
        normed = rms_rows(current_f, norm_gain[0])
        projected = project_rows(
            gathered_rows(normed, "tp", live), weight_zx, weight_bc, weight_dt
        )
        branch_in = mixer_block(
            projected,
            row_ids,
            kernel,
            kernel_bias,
            dt_bias[0],
            a_log[0],
            d_skip[0],
            gated_gain[0],
            live,
        )
        branch = scattered_sum(
            jnp.dot(branch_in, weight_out, preferred_element_type=jnp.float32), "tp", live
        )
        finished = (current_f + branch).astype(jnp.bfloat16)
        saved_slots[0] = jnp.where(micro_index == 0, finished, saved_slots[0])
    stacked = jnp.stack(saved_slots)
    return stacked[None]


def solution(mesh):
    placed = (
        P(None, ("seq", "tp"), None),
        P(None, "seq"),
        P("pipe", None),
        P("pipe", None, None, "tp"),
        P("pipe", None, None),
        P("pipe", None, "tp"),
        P("pipe", None, "tp"),
        P("pipe", None, None),
        P("pipe", "tp"),
        P("pipe", None),
        P("pipe", "tp"),
        P("pipe", "tp"),
        P("pipe", "tp"),
        P("pipe", "tp"),
        P("pipe", "tp", None),
    )
    return jax.shard_map(
        local,
        mesh=mesh,
        in_specs=placed,
        out_specs=P("pipe", None, ("seq", "tp"), None),
        check_vma=False,
    )
```
